32 devices in a mesh: row: 8 (over z, core), col: 4 (over y, x).
Axes of the slice: x: 2, y: 2, z: 4, core: 2. Of those that a mesh axis runs over, the one named last changes fastest.
Arguments:
- potential: float32 [128, 512, 512], P(('row', 'col')), may hold values from -6 to 6
- basis_left: bfloat16 [2048, 128, 384], P(('row', 'col')), may hold values from -1.1953125 to 1.1953125
- basis_right: bfloat16 [2048, 128, 384], P(('row', 'col')), may hold values from -1.1953125 to 1.1953125
- core_matrix: bfloat16 [8192, 8192], P('row', 'col'), may hold values from -3 to 3
- density: bfloat16 [8192, 8192], P('row', 'col'), as said below
- pattern: int32 [64, 64], replicated, may hold values from 0 to 1, as said below
- pair_atoms: int32 [2048, 2], P(('row', 'col')), may hold values from 0 to 63, as said below
- cube_offsets: int32 [2048, 3], P(('row', 'col')), may hold values from 0 to 504, as said below
- live_count: int32 [32], P(('row', 'col')), may hold values from 32 to 64, as said below
Outputs:
- hamiltonian: bfloat16 [8192, 8192], P('row', 'col')
- product: float32 [8192, 8192], P('row', 'col')
The draws below stay inside these ranges and needn't reach their ends.
Inputs may be any that keep to these rules, and one draw needn't show every extreme that they name: `pattern`: symmetric; every diagonal block is 1. density is symmetric. `pair_atoms`: the owner of block (i, j) is (i // 8, j // 16) on a 8 x 4 grid. Among the 64 entry slots of one slab at most 2 name blocks of one owner, and in every draw one owner is named by a live entry of every slab. `cube_offsets`: column 0 is at most 2, column 1 at most 504, column 2 at most 504. `live_count`: some slab uses all its slots.
All inputs are finite; a program needn't handle non-finite values.
Results may differ from the reference program's by a relative error of at most 0.0092.
Values may be sent and summed in bfloat16 or wider, within the bound.
A program may use at most 192 MiB of HBM per device.

```python
import math
import jax
import jax.numpy as jnp
from jax import lax

NB = 128
NATOMS = 64
CX = 4
NY = 512
NZ = 512
E_DEV = 64
HALO = 2
CUBE_X = 6
CUBE = 8
CUBE_CELLS = 384
NBAS = 8192
NX = 128
SLOTS = 2048
N_ROW = 8
N_COL = 4


def broad_shift(key):
    return jax.random.randint(jax.random.fold_in(key, 41), (), 0, NATOMS // N_COL).astype(jnp.int32)


def draw_density(key, part):
    order = NATOMS * NB
    base_key = jax.random.fold_in(key, 5)
    base = jax.random.normal(base_key, (order, order), jnp.float32)
    return ((base + base.T) * (0.70710678 / math.sqrt(order))).astype(jnp.bfloat16)


def draw_pattern(key, part):
    col_atoms = NATOMS // N_COL
    reach = jax.random.randint(jax.random.fold_in(key, 3), (NATOMS,), 1, NATOMS // 4 + 1)
    index = jnp.arange(NATOMS, dtype=jnp.int32)
    reach = jnp.where(index % col_atoms == broad_shift(key), NATOMS // 2, reach)
    apart = jnp.abs(index[:, None] - index[None, :])
    apart = jnp.minimum(apart, NATOMS - apart)
    return (apart <= jnp.maximum(reach[:, None], reach[None, :])).astype(jnp.int32)


def draw_pair_atoms(key, part):
    devices = N_ROW * N_COL
    capacity = (E_DEV + devices - 1) // devices
    hot_owner = jax.random.randint(jax.random.fold_in(key, 7), (), 0, devices)
    slab_keys = jax.random.split(jax.random.fold_in(key, 9), devices)

    def slab_order(slab_key):
        others = capacity + jax.random.permutation(slab_key, devices * capacity - capacity)
        joined = jnp.concatenate([jnp.arange(capacity, dtype=jnp.int32), others.astype(jnp.int32)])
        return joined[:E_DEV]
    orders = jax.vmap(slab_order)(slab_keys)
    owners = (orders + hot_owner * capacity) % (devices * capacity) // capacity
    row_atoms = NATOMS // N_ROW
    col_atoms = NATOMS // N_COL
    local_block = jax.random.randint(jax.random.fold_in(key, 11), (devices, E_DEV), 0, row_atoms * col_atoms)
    first_atom = owners // N_COL * row_atoms + local_block // col_atoms
    second_atom = owners % N_COL * col_atoms + local_block % col_atoms
    slot_index = jnp.arange(E_DEV, dtype=jnp.int32)[None, :]
    broad_atom = owners % N_COL * col_atoms + broad_shift(key)
    second_atom = jnp.where(slot_index < 2, broad_atom, second_atom)
    return jnp.stack([first_atom, second_atom], axis=-1).reshape(devices * E_DEV, 2).astype(jnp.int32)


def draw_cube_offsets(key, part):
    total = N_ROW * N_COL * E_DEV
    top_x = CX + 2 * HALO - CUBE_X
    slot_index = jnp.arange(total, dtype=jnp.int32) % E_DEV
    along_x = jax.random.randint(jax.random.fold_in(key, 19), (total,), 0, top_x + 1)
    along_x = jnp.where(slot_index == 0, 0, jnp.where(slot_index == 1, top_x, along_x))
    along_y = jax.random.randint(jax.random.fold_in(key, 23), (total,), 0, NY - CUBE + 1)
    along_z = jax.random.randint(jax.random.fold_in(key, 29), (total,), 0, NZ - CUBE + 1)
    return jnp.stack([along_x, along_y, along_z], axis=-1).astype(jnp.int32)


def draw_live_count(key, part):
    devices = N_ROW * N_COL
    counts = jax.random.randint(jax.random.fold_in(key, 13), (devices,), E_DEV // 2, E_DEV + 1)
    fullest = jax.random.randint(jax.random.fold_in(key, 17), (), 0, devices)
    return jnp.where(jnp.arange(devices) == fullest, E_DEV, counts).astype(jnp.int32)


def shard_levels(key, dims, cuts, smallest, largest):
    factor_of = 1.0
    for axis_at, parts in cuts:
        heights = jax.random.uniform(jax.random.fold_in(jax.random.fold_in(key, 6), axis_at), (parts,), jnp.float32, smallest / len(cuts), largest / len(cuts))
        factor_of = factor_of * jnp.repeat(jnp.exp(heights), dims[axis_at] // parts).reshape((-1,) + (1,) * (len(dims) - 1 - axis_at))
    return factor_of


def bell_draw(stream_key, shape, deviation, bound, cuts=(), kind=jnp.bfloat16):
    entries = deviation * jax.random.normal(stream_key, shape, jnp.float32)
    if cuts:
        entries = entries * shard_levels(stream_key, shape, cuts, -0.22, 0.18)
    return jnp.clip(entries, -bound, bound).astype(kind)


def setup_inputs(seed: int = 0) -> dict:
    key_list = jax.random.split(jax.random.key(seed), 10)
    return {
        "potential": bell_draw(key_list[0], (NX, NY, NZ), 1.0, 6.0, ((0, 32),), jnp.float32),
        "basis_left": bell_draw(key_list[1], (SLOTS, NB, CUBE_CELLS), 0.2, 1.1953125, ((0, 32),)),
        "basis_right": bell_draw(key_list[2], (SLOTS, NB, CUBE_CELLS), 0.2, 1.1953125, ((0, 32),)),
        "core_matrix": bell_draw(key_list[3], (NBAS, NBAS), 0.5, 3.0, ((0, 8), (1, 4))),
        "density": draw_density(jax.random.fold_in(key_list[9], 71), 0),
        "pattern": draw_pattern(jax.random.fold_in(key_list[9], 71), 0),
        "pair_atoms": draw_pair_atoms(jax.random.fold_in(key_list[9], 71), 0),
        "cube_offsets": draw_cube_offsets(jax.random.fold_in(key_list[9], 71), 0),
        "live_count": draw_live_count(jax.random.fold_in(key_list[9], 71), 0),
    }


HIGHEST = lax.Precision.HIGHEST


def block_mask(values, pattern_tile, block_size):
    row_blocks, col_blocks = pattern_tile.shape
    shaped = values.reshape(row_blocks, block_size, col_blocks, block_size)
    selected = (pattern_tile > 0)[:, None, :, None]
    kept = jnp.where(selected, shaped, jnp.zeros((), values.dtype))
    return kept.reshape(row_blocks * block_size, col_blocks * block_size)


def reference(potential, basis_left, basis_right, core_matrix, density, pattern, pair_atoms, cube_offsets, live_count):
    devices = N_ROW * N_COL
    slab_planes = NX // devices
    slot_total = pair_atoms.shape[0]
    per_slab = slot_total // devices
    ordinal = jnp.arange(slot_total, dtype=jnp.int32)
    slab_index = ordinal // per_slab
    live_flag = ((ordinal % per_slab) < live_count[slab_index]).astype(jnp.float32)

    def integrate(entry):
        left_table, right_table, offsets, slab_number, flag_value = entry
        planes = (slab_number * slab_planes - HALO + offsets[0] + jnp.arange(CUBE_X, dtype=jnp.int32)) % NX
        slab_rows = jnp.take(potential, planes.astype(jnp.int32), axis=0)
        start = (jnp.zeros((), jnp.int32), offsets[1].astype(jnp.int32), offsets[2].astype(jnp.int32))
        cube_cells = lax.dynamic_slice(slab_rows, start, (CUBE_X, CUBE, CUBE)).reshape(-1)
        weighted = (left_table.astype(jnp.float32) * cube_cells[None, :]).astype(jnp.bfloat16)
        block_value = jnp.dot(weighted.astype(jnp.float32), right_table.astype(jnp.float32).T, precision=HIGHEST)
        return block_value * flag_value

    partials = lax.map(integrate, (basis_left, basis_right, cube_offsets, slab_index, live_flag))
    block_id = (pair_atoms[:, 0] * NATOMS + pair_atoms[:, 1]).astype(jnp.int32)
    summed = jax.ops.segment_sum(partials, block_id, num_segments=NATOMS * NATOMS)
    integrals = summed.reshape(NATOMS, NATOMS, NB, NB).transpose(0, 2, 1, 3).reshape(NATOMS * NB, NATOMS * NB)
    hamiltonian = block_mask(core_matrix.astype(jnp.float32) + integrals, pattern, NB).astype(jnp.bfloat16)
    masked_density = block_mask(density, pattern, NB)
    product = jnp.dot(hamiltonian.astype(jnp.float32), masked_density.astype(jnp.float32), precision=HIGHEST)
    return hamiltonian, product
```

```python
import functools

import jax
import jax.numpy as jnp
from jax import lax
from jax.experimental import pallas as pl
from jax.experimental.pallas import tpu as pltpu
from jax.sharding import PartitionSpec as P

NATOMS = 64
HALO = 2
CUBE_X = 6
CUBE = 8
LANES = 128
GROUP = 8


def cut_kernel(ys, zs, grid_ref, out_ref):
    planes, height, depth = grid_ref.shape
    rows = planes * CUBE
    cells = rows * CUBE
    spread = (
        lax.broadcasted_iota(jnp.int32, (LANES, cells), 1) % CUBE
        == lax.broadcasted_iota(jnp.int32, (LANES, cells), 0)
    ).astype(jnp.float32)
    own = (
        lax.broadcasted_iota(jnp.int32, (rows, cells), 1) // CUBE
        == lax.broadcasted_iota(jnp.int32, (rows, cells), 0)
    )

    def step(g, carry):
        pieces = []
        for t in range(GROUP):
            y = ys[g * GROUP + t]
            z = zs[g * GROUP + t]
            top = pl.multiple_of(jnp.minimum(y // CUBE * CUBE, height - 2 * CUBE), CUBE)
            base = pl.multiple_of(jnp.minimum(z // LANES * LANES, depth - 2 * LANES), LANES)
            window = grid_ref[:, pl.ds(top, 2 * CUBE), pl.ds(base, 2 * LANES)]
            window = pltpu.roll(window, lax.rem(2 * CUBE - (y - top), 2 * CUBE), 1)
            window = window[:, :CUBE].reshape(rows, 2 * LANES)
            window = pltpu.roll(window, lax.rem(2 * LANES - (z - base), 2 * LANES), 1)
            pieces.append(window[:, :LANES])
        stacked = jnp.concatenate(pieces, axis=0)
        wide = jnp.dot(
            stacked, spread, precision=lax.Precision.HIGHEST, preferred_element_type=jnp.float32
        )
        wide = jnp.where(own[None], wide.reshape(GROUP, rows, cells), 0.0)
        out_ref[pl.ds(pl.multiple_of(g * GROUP, GROUP), GROUP), :] = jnp.sum(wide, axis=1)
        return carry

    lax.fori_loop(0, out_ref.shape[0] // GROUP, step, 0)


def cut_pieces(potential, ys, zs):
    items = ys.shape[0]
    cells = potential.shape[0] * CUBE * CUBE
    return pl.pallas_call(
        cut_kernel,
        out_shape=jax.ShapeDtypeStruct((items, cells), jnp.float32),
        in_specs=[
            pl.BlockSpec(memory_space=pltpu.SMEM),
            pl.BlockSpec(memory_space=pltpu.SMEM),
            pl.BlockSpec(memory_space=pltpu.VMEM),
        ],
        out_specs=pl.BlockSpec(memory_space=pltpu.VMEM),
        cost_estimate=pl.CostEstimate(
            flops=items * cells * 4096, bytes_accessed=potential.size * 4, transcendentals=0
        ),
        name="cut_pieces",
    )(ys, zs, potential)


def block_kernel(fill, placed, left_ref, right_ref, cube_ref, out_ref):
    step = pl.program_id(0)
    if fill:

        @pl.when(step == 0)
        def _():
            out_ref[...] = jnp.zeros_like(out_ref)

    cubes = cube_ref[...]
    for t in range(GROUP):
        weighted = (left_ref[t].astype(jnp.float32) * cubes[t : t + 1, :]).astype(jnp.bfloat16)
        block = lax.dot_general(
            weighted,
            right_ref[t],
            (((1,), (1,)), ((), ())),
            preferred_element_type=jnp.float32,
        )
        out_ref[placed[step * GROUP + t]] = block.astype(out_ref.dtype)


def make_blocks(placed, basis_left, basis_right, cubes, slots):
    entries, size, cells = basis_left.shape
    table = pl.BlockSpec((GROUP, size, cells), lambda s, placed: (s, 0, 0))
    return pl.pallas_call(
        functools.partial(block_kernel, slots > entries),
        out_shape=jax.ShapeDtypeStruct((slots, size, size), jnp.bfloat16),
        grid_spec=pltpu.PrefetchScalarGridSpec(
            num_scalar_prefetch=1,
            grid=(entries // GROUP,),
            in_specs=[table, table, pl.BlockSpec((GROUP, cells), lambda s, placed: (s, 0))],
            out_specs=pl.BlockSpec((slots, size, size), lambda s, placed: (0, 0, 0)),
        ),
        cost_estimate=pl.CostEstimate(
            flops=2 * entries * size * size * cells,
            bytes_accessed=4 * entries * size * cells,
            transcendentals=0,
        ),
        name="make_blocks",
    )(placed, basis_left, basis_right, cubes)


def build_kernel(ids, tile, core_ref, received_ref, out_ref, total):
    size = received_ref.shape[1]
    row_blocks = core_ref.shape[0] // size
    col_blocks = core_ref.shape[1] // size

    def load(i, carry):
        rows = pl.ds(pl.multiple_of(i * size, size), size)
        for j in range(col_blocks):
            total[i * col_blocks + j] = core_ref[rows, j * size : (j + 1) * size].astype(
                jnp.float32
            )
        return carry

    lax.fori_loop(0, row_blocks, load, 0)

    def add(s, carry):
        where_to = ids[s]

        @pl.when(where_to >= 0)
        def _():
            total[where_to] += received_ref[s].astype(jnp.float32)

        return carry

    lax.fori_loop(0, received_ref.shape[0], add, 0)

    def store(i, carry):
        rows = pl.ds(pl.multiple_of(i * size, size), size)
        for j in range(col_blocks):
            kept = jnp.full((size, size), tile[i * col_blocks + j], jnp.int32) > 0
            out_ref[rows, j * size : (j + 1) * size] = jnp.where(
                kept, total[i * col_blocks + j], 0.0
            ).astype(out_ref.dtype)
        return carry

    lax.fori_loop(0, row_blocks, store, 0)


def build_matrix(ids, tile, core_matrix, received):
    size = received.shape[1]
    blocks = core_matrix.size // (size * size)
    vmem = pl.BlockSpec(memory_space=pltpu.VMEM)
    smem = pl.BlockSpec(memory_space=pltpu.SMEM)
    return pl.pallas_call(
        build_kernel,
        out_shape=jax.ShapeDtypeStruct(core_matrix.shape, jnp.bfloat16),
        in_specs=[smem, smem, vmem, vmem],
        out_specs=vmem,
        scratch_shapes=[pltpu.VMEM((blocks, size, size), jnp.float32)],
        cost_estimate=pl.CostEstimate(
            flops=4 * core_matrix.size, bytes_accessed=16 * core_matrix.size, transcendentals=0
        ),
        name="build_matrix",
    )(ids, tile, core_matrix, received)


def block_mask(values, pattern_tile, block_size):
    row_blocks, col_blocks = pattern_tile.shape
    shaped = values.reshape(row_blocks, block_size, col_blocks, block_size)
    selected = (pattern_tile > 0)[:, None, :, None]
    kept = jnp.where(selected, shaped, jnp.zeros((), values.dtype))
    return kept.reshape(row_blocks * block_size, col_blocks * block_size)


def ring_gather(block, axis, rings):
    count = len(rings[0])
    up = [(ring[i], ring[(i + 1) % count]) for ring in rings for i in range(count)]
    down = [(j, i) for i, j in up]
    found = []
    rising, falling = block, block
    for distance in range(1, count // 2 + 1):
        rows = block.shape[0]
        half = rows // 2
        if 2 * distance < count:
            rising = lax.ppermute(rising, axis, up)
            falling = lax.ppermute(falling, axis, down)
            found.append((distance, 0, rising))
            found.append((count - distance, 0, falling))
        else:
            found.append((distance, 0, lax.ppermute(rising[:half], axis, up)))
            found.append((distance, half, lax.ppermute(falling[half:], axis, down)))
    return found


def shards(
    potential,
    basis_left,
    basis_right,
    core_matrix,
    density,
    pattern,
    pair_atoms,
    cube_offsets,
    live_count,
):
    row_count = lax.axis_size("row")
    col_count = lax.axis_size("col")
    devices = row_count * col_count
    row_index = lax.axis_index("row")
    col_index = lax.axis_index("col")
    block_size = basis_left.shape[1]
    entries = pair_atoms.shape[0]
    atom_rows = NATOMS // row_count
    atom_cols = NATOMS // col_count
    capacity = (entries + devices - 1) // devices
    slot_total = devices * capacity
    both = ("row", "col")
    up = [(i, (i + 1) % devices) for i in range(devices)]
    down = [(j, i) for i, j in up]

    asked = cube_offsets[:, 1:].T.reshape(-1)
    from_before = lax.ppermute(asked, both, up)
    from_after = lax.ppermute(asked, both, down)
    ys = jnp.concatenate([asked[:entries], from_before[:entries], from_after[:entries]])
    zs = jnp.concatenate([asked[entries:], from_before[entries:], from_after[entries:]])

    corner = (row_index * atom_rows, col_index * atom_cols)
    pattern_tile = lax.dynamic_slice(pattern, corner, (atom_rows, atom_cols))
    masked_density = block_mask(density, pattern_tile, block_size)

    depth, width = masked_density.shape
    chips = row_count // 2
    rings = [[2 * z + core for z in range(chips)] for core in range(2)]
    swap = [(i, i ^ 1) for i in range(row_count)]
    column = jnp.zeros((row_count * depth, width), masked_density.dtype)
    chip, core = row_index // 2, row_index % 2
    pieces = [(0, 0, masked_density)] + ring_gather(masked_density, "row", rings)
    for back, first, piece in pieces:
        origin = lax.rem(chip - back + chips, chips) * 2
        other = lax.ppermute(piece, "row", swap)
        column = lax.dynamic_update_slice(column, piece, ((origin + core) * depth + first, 0))
        column = lax.dynamic_update_slice(column, other, ((origin + 1 - core) * depth + first, 0))

    ordinal = jnp.arange(entries, dtype=jnp.int32)
    first_atom = pair_atoms[:, 0]
    second_atom = pair_atoms[:, 1]
    owner_index = first_atom // atom_rows * col_count + second_atom // atom_cols
    local_block = first_atom % atom_rows * atom_cols + second_atom % atom_cols
    local_block = jnp.where(ordinal < live_count[0], local_block, -1)
    earlier = (owner_index[:, None] == owner_index[None, :]) & (ordinal[None, :] < ordinal[:, None])
    placed = owner_index * capacity + jnp.sum(earlier.astype(jnp.int32), axis=1)
    sending = placed[None, :] == jnp.arange(slot_total, dtype=jnp.int32)[:, None]
    outgoing_ids = jnp.sum(jnp.where(sending, local_block[None, :] + 1, 0), axis=1) - 1
    received_ids = lax.all_to_all(
        outgoing_ids.reshape(devices, capacity), both, split_axis=0, concat_axis=0, tiled=True
    ).reshape(slot_total)

    cut = cut_pieces(potential, ys, zs)
    halo_cells = HALO * CUBE * CUBE
    after = lax.ppermute(cut[entries : 2 * entries, :halo_cells], both, down)
    before = lax.ppermute(cut[2 * entries :, -halo_cells:], both, up)
    padded = jnp.concatenate([before, cut[:entries], after], axis=1)
    plane, cells = CUBE * CUBE, CUBE_X * CUBE * CUBE
    cubes = padded[:, :cells]
    for shift in range(1, (padded.shape[1] - cells) // plane + 1):
        cubes = jnp.where(
            cube_offsets[:, :1] == shift, padded[:, shift * plane : shift * plane + cells], cubes
        )

    outgoing = make_blocks(placed, basis_left, basis_right, cubes, slot_total)
    received = lax.all_to_all(outgoing, both, split_axis=0, concat_axis=0, tiled=True)
    hamiltonian = build_matrix(received_ids, pattern_tile.reshape(-1), core_matrix, received)

    order = [i for i in range(0, col_count, 2)] + [i for i in range(1, col_count, 2)][::-1]
    spot = [order.index(i) for i in range(col_count)]
    place = jnp.array(spot, jnp.int32)[col_index]
    ordered = jnp.array(order, jnp.int32)
    found = ring_gather(hamiltonian, "col", [order])

    def multiply(block, back):
        origin = ordered[lax.rem(place - back + col_count, col_count)]
        part = lax.dynamic_slice(column, (origin * block.shape[1], 0), (block.shape[1], width))
        return jnp.dot(block, part, preferred_element_type=jnp.float32)

    product = multiply(hamiltonian, 0)
    halves = {}
    for back, first, block in found:
        if block.shape[0] == hamiltonian.shape[0]:
            product = product + multiply(block, back)
        else:
            halves.setdefault(back, {})[first] = block
    for back, parts in halves.items():
        block = jnp.concatenate([parts[first] for first in sorted(parts)], axis=0)
        product = product + multiply(block, back)
    return (hamiltonian, product)


def solution(mesh):
    in_specs = (
        P(("row", "col"), None, None),
        P(("row", "col"), None, None),
        P(("row", "col"), None, None),
        P("row", "col"),
        P("row", "col"),
        P(),
        P(("row", "col"), None),
        P(("row", "col"), None),
        P(("row", "col")),
    )
    out_specs = (P("row", "col"), P("row", "col"))
    return jax.shard_map(shards, mesh=mesh, in_specs=in_specs, out_specs=out_specs, check_vma=False)
```
